32 devices in a mesh: tm: 4 (over y, x), tmpl: 8 (over z, core).
Axes of the slice: x: 2, y: 2, z: 4, core: 2. Of those that a mesh axis runs over, the one named last changes fastest.
Arguments:
- strain: float32 [3, 2048], P(None, 'tm'), may hold values from -21 to 21
- gate_lengths: int32 [16], replicated, may hold values from 1 to 256, 2048 in all
- filters: bfloat16 [8, 1024, 512], P('tmpl'), may hold values from -0.1875 to 0.1875
- mixing: bfloat16 [512, 2, 8192], P(None, None, 'tmpl'), may hold values from -2 to 2
Outputs:
- marginal: float32 [2048], P('tm')
The draws below stay inside these ranges and needn't reach their ends.
Inputs may be any that keep to these rules, and one draw needn't show every extreme that they name: `gate_lengths`: the 16 lengths sum to 2048; the largest is exactly 256.
All inputs are finite; a program needn't handle non-finite values.
Results may differ from the reference program's by a relative error of at most 0.0019.
Values may be sent and summed in bfloat16 or wider, within the bound.
A program may use at most 64 MiB of HBM per device.

```python
import math
import jax
import jax.numpy as jnp
import numpy as np
from jax import lax

DET = 3
NB = 512
TAPS = 1024
GATES = 16
TPL_DEV = 1024
SAMPLES = 2048
SUBBANKS = 8


def draw_strain(key, part):
    noise_key = jax.random.fold_in(key, 0)
    return jnp.clip(jax.random.normal(noise_key, (DET, SAMPLES), jnp.float32), -6.0, 6.0)


def draw_mixing(key, part):
    shared_key, own_key = jax.random.split(jax.random.fold_in(key, 7), 2)
    shared = jnp.clip(jax.random.normal(shared_key, (NB, 2, SUBBANKS, 1), jnp.float32), -4.0, 4.0)
    own = jnp.clip(jax.random.normal(own_key, (NB, 2, SUBBANKS, TPL_DEV), jnp.float32), -4.0, 4.0)
    mixed = (0.83666 * shared + 0.5477226 * own) / math.sqrt(NB)
    return mixed.reshape(NB, 2, SUBBANKS * TPL_DEV).astype(jnp.bfloat16)


def block_levels(stream_key, extent, cuts, least, high):
    def one(dim, shards_of):
        heights = jax.random.uniform(jax.random.fold_in(jax.random.fold_in(stream_key, 6), dim), (shards_of,), jnp.float32, least / len(cuts), high / len(cuts))
        return jnp.repeat(jnp.exp(heights), extent[dim] // shards_of).reshape((-1,) + (1,) * (len(extent) - dim - 1))

    level = one(*cuts[0])
    for cut in cuts[1:]:
        level = level * one(*cut)
    return level


def length_profile(number_of, total, reach, slope):
    portions = [(1 << 20) // math.isqrt(grade ** slope) + 1 for grade in range(2, number_of + 1)]
    surplus, counts = total - reach - (number_of - 1), [1] * (number_of - 1)
    while surplus > 0:
        movable = [i for i in range(number_of - 1) if counts[i] < reach]
        whole, left = sum([portions[i] for i in movable]), surplus
        for i in movable:
            more = min(reach - counts[i], max(1, left * portions[i] // whole), surplus)
            counts[i] = counts[i] + more
            surplus = surplus - more
    return np.array([reach] + counts)


def uneven_parts(stream_key, number_of, total, bound, slope):
    if number_of == 2:
        one = jax.random.randint(stream_key, (), max(1, total - bound), min(bound, total - 1) + 1)
        return jnp.stack([one, total - one])
    tallies = jnp.asarray(length_profile(number_of, total, bound, slope), jnp.int32)
    twos = (number_of - 1) // 2
    giver, taker = tallies[1:1 + 2 * twos:2], tallies[2:2 + 2 * twos:2]
    margin = jnp.minimum(giver - 1, bound - taker)
    moved = jax.random.randint(jax.random.fold_in(stream_key, 1), (twos,), 0, 1 << 20) % (margin + 1)
    tallies = tallies.at[1:1 + 2 * twos:2].set(giver - moved).at[2:2 + 2 * twos:2].set(taker + moved)
    return tallies[jax.random.permutation(jax.random.fold_in(stream_key, 2), number_of)]


def scatter_about(key, shape, spread, bound, cuts=(), kind=jnp.bfloat16):
    drawn = spread * jax.random.normal(key, shape, jnp.float32)
    if cuts:
        drawn = drawn * block_levels(key, shape, cuts, -0.22, 0.18)
    return jnp.clip(drawn, -bound, bound).astype(kind)


def setup_inputs(seed: int = 0) -> dict:
    key_list = jax.random.split(jax.random.key(seed), 5)
    strain = draw_strain(jax.random.fold_in(key_list[4], 71), 0)
    gate_lengths = uneven_parts(key_list[1], GATES, SAMPLES, SAMPLES // 8, 1).astype(jnp.int32)
    filters = scatter_about(key_list[2], (SUBBANKS, TAPS, NB), TAPS ** -0.5, 0.1875, ((0, 8),))
    mixing = draw_mixing(jax.random.fold_in(key_list[4], 71), 0)
    return {"strain": strain, "gate_lengths": gate_lengths, "filters": filters, "mixing": mixing}


def apply_gates(strain, gate_lengths, positions):
    bounds = jnp.cumsum(gate_lengths).astype(jnp.int32)
    passed = jnp.sum((bounds[None, :] <= positions[:, None]).astype(jnp.int32), axis=1)
    keep = (passed % 2 == 0).astype(jnp.float32)
    return strain * keep[None, :]


def reference(strain, gate_lengths, filters, mixing):
    det_count, sample_count = strain.shape
    positions = jnp.arange(sample_count, dtype=jnp.int32)
    gated = apply_gates(strain, gate_lengths, positions).astype(jnp.bfloat16)
    tap_count = filters.shape[1]
    basis_width = filters.shape[2]
    padded = jnp.pad(gated.astype(jnp.float32), ((0, 0), (tap_count - 1, 0)))[:, :, None]
    per_bank = mixing.reshape(basis_width, 2, SUBBANKS, TPL_DEV).transpose(2, 0, 1, 3).reshape(SUBBANKS, basis_width, 2 * TPL_DEV)

    def one_bank(inputs):
        bank_filters, bank_mixing = inputs
        basis = lax.conv_general_dilated(padded, bank_filters.astype(jnp.float32)[:, None, :], (1,), "VALID", dimension_numbers=("NWC", "WIO", "NWC"), precision=lax.Precision.HIGHEST)
        rounded = lax.optimization_barrier(basis.astype(jnp.bfloat16))
        flat = rounded.astype(jnp.float32).reshape(-1, basis_width)
        signal = jnp.dot(flat, bank_mixing.astype(jnp.float32), precision=lax.Precision.HIGHEST)
        signal = signal.reshape(det_count, sample_count, 2, TPL_DEV)
        scores = 0.5 * jnp.sum(signal * signal, axis=(0, 2))
        bank_peak = jnp.max(scores, axis=1)
        bank_total = jnp.sum(jnp.exp(scores - bank_peak[:, None]), axis=1)
        return bank_peak, bank_total

    peaks, totals = lax.map(one_bank, (filters, per_bank))
    overall = jnp.max(peaks, axis=0)
    total = jnp.sum(totals * jnp.exp(peaks - overall[None, :]), axis=0)
    return overall + jnp.log(total) - math.log(SUBBANKS * TPL_DEV)
```

```python
import functools
import math

import jax
import jax.numpy as jnp
from jax import lax
from jax.experimental import pallas as pl
from jax.experimental.pallas import tpu as pltpu
from jax.sharding import PartitionSpec as P

MESH = pl.DeviceIdType.MESH
LANES = 128
ROWS = 8


def kernel(
    tm_count,
    tmpl_count,
    strain_ref,
    gates_ref,
    filters_hbm,
    mixing_hbm,
    out_ref,
    filters_ref,
    mixing_ref,
    ext_ref,
    hankel_ref,
    basis_ref,
    score_ref,
    gather_ref,
    load_sems,
    halo_send,
    halo_recv,
    out_send,
    out_recv,
):
    dets, seg = strain_ref.shape
    taps, width = filters_ref.shape
    templates = mixing_ref.shape[2]
    hops = (taps + seg - 2) // seg
    tm = lax.axis_index("tm")
    tmpl = lax.axis_index("tmpl")

    loads = [
        pltpu.make_async_copy(filters_hbm.at[0], filters_ref, load_sems.at[0]),
        pltpu.make_async_copy(mixing_hbm, mixing_ref, load_sems.at[1]),
    ]
    for load in loads:
        load.start()

    barrier = pltpu.get_barrier_semaphore()
    reach = sorted({o % tm_count for h in range(1, hops + 1) for o in (h, -h)} - {0})
    for o in reach:
        pl.semaphore_signal(
            barrier, inc=1, device_id=(lax.rem(tm + o, tm_count), tmpl), device_id_type=MESH
        )
    for o in range(1, tmpl_count):
        pl.semaphore_signal(
            barrier, inc=1, device_id=(tm, lax.rem(tmpl + o, tmpl_count)), device_id_type=MESH
        )

    positions = tm * seg + lax.broadcasted_iota(jnp.int32, (1, seg), 1)
    passed = jnp.zeros((1, seg), jnp.int32)
    bound = jnp.int32(0)
    for g in range(gates_ref.shape[0]):
        bound = bound + gates_ref[g]
        passed = passed + (bound <= positions).astype(jnp.int32)
    keep = ((passed & 1) == 0).astype(jnp.float32)
    ext_ref[hops] = (strain_ref[...] * keep).astype(jnp.bfloat16).astype(jnp.float32)

    pl.semaphore_wait(barrier, len(reach) + tmpl_count - 1)
    halos = []
    for h in range(1, hops + 1):
        halo = pltpu.make_async_remote_copy(
            src_ref=ext_ref.at[hops],
            dst_ref=ext_ref.at[hops - h],
            send_sem=halo_send.at[h - 1],
            recv_sem=halo_recv.at[h - 1],
            device_id=(lax.rem(tm + h, tm_count), tmpl),
            device_id_type=MESH,
        )
        halo.start()
        halos.append(halo)

    per_piece = seg // LANES
    blocks = (hops + 1) * per_piece
    row = lax.broadcasted_iota(jnp.int32, (ROWS, LANES), 0)
    lane = lax.broadcasted_iota(jnp.int32, (ROWS, LANES), 1)
    inside = [lane + row + (r + 1) < LANES for r in range(0, LANES, ROWS)]

    def skewed(d, m):
        piece = m // per_piece
        at = (m % per_piece) * LANES
        line = ext_ref[piece, d : d + 1, at : at + LANES]
        if piece < hops:
            line = jnp.where(tm >= hops - piece, line, 0.0)
        wide = jnp.broadcast_to(line, (ROWS, LANES))
        tilted = pltpu.roll(wide, LANES - 1, 1)
        for bit in (1, 2, 4):
            tilted = jnp.where((row & bit) == 0, tilted, pltpu.roll(tilted, LANES - bit, 1))
        return [tilted if r == 0 else pltpu.roll(tilted, LANES - r, 1) for r in range(0, LANES, ROWS)]

    def fill(d, first, last):
        now = skewed(d, first)
        for m in range(first, last):
            later = skewed(d, m + 1)
            tiles = [jnp.where(i, a, b) for i, a, b in zip(inside, now, later)]
            hankel_ref[d, m * LANES : (m + 1) * LANES, :] = jnp.concatenate(tiles, axis=0).astype(
                jnp.bfloat16
            )
            now = later

    own = hops * per_piece
    for d in range(dets):
        fill(d, own, blocks - 1)
    for load in loads:
        load.wait()
    for halo in halos:
        halo.wait()
    for d in range(dets):
        fill(d, 0, own)
        windows = jnp.concatenate(
            [hankel_ref[d, k : k + seg, :] for k in range(0, taps, LANES)], axis=1
        )
        basis = jnp.dot(windows, filters_ref[...], preferred_element_type=jnp.float32)
        basis_ref[d] = basis.astype(jnp.bfloat16)

    step = 256
    for j in range(0, templates, step):
        total = None
        for d in range(dets):
            for c in range(2):
                signal = jnp.dot(
                    basis_ref[d],
                    mixing_ref[c, :, j : j + step],
                    preferred_element_type=jnp.float32,
                )
                total = signal * signal if total is None else total + signal * signal
        score_ref[:, j : j + step] = 0.5 * total

    for t in range(0, seg, LANES):
        tiles = [score_ref[t : t + LANES, j : j + LANES] for j in range(0, templates, LANES)]
        peak = functools.reduce(jnp.maximum, tiles)
        mass = functools.reduce(jnp.add, [jnp.exp(tile - peak) for tile in tiles])
        peak, mass = peak.T, mass.T
        top = jnp.max(peak, axis=0, keepdims=True)
        mass = jnp.sum(mass * jnp.exp(peak - top), axis=0, keepdims=True)
        gather_ref[tmpl, :, t : t + LANES] = top + jnp.log(mass)

    sends = []
    for o in range(1, tmpl_count):
        send = pltpu.make_async_remote_copy(
            src_ref=gather_ref.at[tmpl],
            dst_ref=gather_ref.at[tmpl],
            send_sem=out_send.at[o],
            recv_sem=out_recv.at[o],
            device_id=(tm, lax.rem(tmpl + o, tmpl_count)),
            device_id_type=MESH,
        )
        send.start()
        sends.append(send)
    for send in sends:
        send.wait()
    parts = [gather_ref[i] for i in range(tmpl_count)]
    top = functools.reduce(jnp.maximum, parts)
    mass = functools.reduce(jnp.add, [jnp.exp(part - top) for part in parts])
    out_ref[...] = top + jnp.log(mass) - math.log(templates * tmpl_count)


def shards(tm_count, tmpl_count, strain, gate_lengths, filters, mixing):
    dets, seg = strain.shape
    _, taps, width = filters.shape
    templates = mixing.shape[2]
    hops = (taps + seg - 2) // seg
    mixing = mixing.transpose(1, 0, 2)
    out = pl.pallas_call(
        functools.partial(kernel, tm_count, tmpl_count),
        out_shape=jax.ShapeDtypeStruct((1, seg), jnp.float32),
        in_specs=[
            pl.BlockSpec(memory_space=pltpu.VMEM),
            pl.BlockSpec(memory_space=pltpu.SMEM),
            pl.BlockSpec(memory_space=pl.ANY),
            pl.BlockSpec(memory_space=pl.ANY),
        ],
        out_specs=pl.BlockSpec(memory_space=pltpu.VMEM),
        scratch_shapes=[
            pltpu.VMEM((taps, width), jnp.bfloat16),
            pltpu.VMEM((2, width, templates), jnp.bfloat16),
            pltpu.VMEM((hops + 1, dets, seg), jnp.float32),
            pltpu.VMEM((dets, hops * seg + seg - LANES, LANES), jnp.bfloat16),
            pltpu.VMEM((dets, seg, width), jnp.bfloat16),
            pltpu.VMEM((seg, templates), jnp.float32),
            pltpu.VMEM((tmpl_count, 1, seg), jnp.float32),
            pltpu.SemaphoreType.DMA((2,)),
            pltpu.SemaphoreType.DMA((hops,)),
            pltpu.SemaphoreType.DMA((hops,)),
            pltpu.SemaphoreType.DMA((tmpl_count,)),
            pltpu.SemaphoreType.DMA((tmpl_count,)),
        ],
        compiler_params=pltpu.CompilerParams(
            collective_id=0, has_side_effects=True, vmem_limit_bytes=40 * 2**20
        ),
    )(strain, gate_lengths, filters, mixing)
    return out.reshape(seg)


def solution(mesh):
    body = functools.partial(shards, mesh.shape["tm"], mesh.shape["tmpl"])
    in_specs = (P(None, "tm"), P(), P("tmpl", None, None), P(None, None, "tmpl"))
    return jax.shard_map(body, mesh=mesh, in_specs=in_specs, out_specs=P("tm"), check_vma=False)
```

```python
import functools
import math

import jax
import jax.numpy as jnp
from jax import lax
from jax.experimental import pallas as pl
from jax.experimental.pallas import tpu as pltpu
from jax.sharding import PartitionSpec as P

MESH = pl.DeviceIdType.MESH
LANES = 128
ROWS = 8
CHUNKS = 4


def kernel(
    tm_count,
    tmpl_count,
    strain_hbm,
    gates_hbm,
    filters_hbm,
    mixing_hbm,
    out_ref,
    strain_ref,
    gates_ref,
    filters_ref,
    raw_ref,
    mixing_ref,
    ext_ref,
    hankel_ref,
    basis_ref,
    score_ref,
    gather_ref,
    load_sems,
    halo_send,
    halo_recv,
    out_send,
    out_recv,
):
    dets, seg = strain_ref.shape
    taps, width = filters_ref.shape
    templates = mixing_ref.shape[2]
    hops = (taps + seg - 2) // seg
    tm = lax.axis_index("tm")
    tmpl = lax.axis_index("tmpl")

    barrier = pltpu.get_barrier_semaphore()
    reach = sorted({o % tm_count for h in range(1, hops + 1) for o in (h, -h)} - {0})
    for o in reach:
        pl.semaphore_signal(
            barrier, inc=1, device_id=(lax.rem(tm + o, tm_count), tmpl), device_id_type=MESH
        )
    for o in range(1, tmpl_count):
        pl.semaphore_signal(
            barrier, inc=1, device_id=(tm, lax.rem(tmpl + o, tmpl_count)), device_id_type=MESH
        )

    small = [
        pltpu.make_async_copy(strain_hbm, strain_ref, load_sems.at[0]),
        pltpu.make_async_copy(gates_hbm, gates_ref, load_sems.at[1]),
    ]
    chunk = width // CHUNKS
    mixing_loads = [
        pltpu.make_async_copy(
            mixing_hbm.at[pl.ds(i * chunk, chunk)],
            raw_ref.at[pl.ds(i * chunk, chunk)],
            load_sems.at[3 + i],
        )
        for i in range(CHUNKS)
    ]
    filters_load = pltpu.make_async_copy(filters_hbm.at[0], filters_ref, load_sems.at[2])
    for load in small + mixing_loads + [filters_load]:
        load.start()
    for load in small:
        load.wait()

    positions = tm * seg + lax.broadcasted_iota(jnp.int32, (1, seg), 1)
    passed = jnp.zeros((1, seg), jnp.int32)
    bound = jnp.int32(0)
    for g in range(gates_ref.shape[0]):
        bound = bound + gates_ref[g]
        passed = passed + (bound <= positions).astype(jnp.int32)
    keep = ((passed & 1) == 0).astype(jnp.float32)
    ext_ref[hops] = (strain_ref[...] * keep).astype(jnp.bfloat16).astype(jnp.float32)

    pl.semaphore_wait(barrier, len(reach) + tmpl_count - 1)
    halos = []
    for h in range(1, hops + 1):
        halo = pltpu.make_async_remote_copy(
            src_ref=ext_ref.at[hops],
            dst_ref=ext_ref.at[hops - h],
            send_sem=halo_send.at[h - 1],
            recv_sem=halo_recv.at[h - 1],
            device_id=(lax.rem(tm + h, tm_count), tmpl),
            device_id_type=MESH,
        )
        halo.start()
        halos.append(halo)

    per_piece = seg // LANES
    blocks = (hops + 1) * per_piece
    row = lax.broadcasted_iota(jnp.int32, (ROWS, LANES), 0)
    lane = lax.broadcasted_iota(jnp.int32, (ROWS, LANES), 1)
    inside = [lane - row + (r + ROWS) < LANES for r in range(0, LANES, ROWS)]

    def skewed(d, m):
        piece = m // per_piece
        at = (m % per_piece) * LANES
        line = ext_ref[piece, d : d + 1, at : at + LANES]
        if piece < hops:
            line = jnp.where(tm >= hops - piece, line, 0.0)
        wide = jnp.broadcast_to(line, (ROWS, LANES))
        return [
            pltpu.roll(wide, LANES - ROWS - r, 1, stride=1, stride_axis=0)
            for r in range(0, LANES, ROWS)
        ]

    def fill(d, first, last):
        now = skewed(d, first)
        for m in range(first, last):
            later = skewed(d, m + 1)
            tiles = [jnp.where(i, a, b) for i, a, b in zip(inside, now, later)]
            hankel_ref[d, m * LANES : (m + 1) * LANES, :] = jnp.concatenate(tiles, axis=0).astype(
                jnp.bfloat16
            )
            now = later

    own = hops * per_piece
    for d in range(dets):
        fill(d, own, blocks - 1)
    for i, load in enumerate(mixing_loads):
        load.wait()
        part = jnp.swapaxes(raw_ref[i * chunk : (i + 1) * chunk], 0, 1)
        for c in range(2):
            mixing_ref[c, i * chunk : (i + 1) * chunk, :] = part[c]
    filters_load.wait()
    for halo in halos:
        halo.wait()
    for d in range(dets):
        fill(d, 0, own)
        windows = jnp.concatenate(
            [hankel_ref[d, k : k + seg, :] for k in range(0, taps, LANES)], axis=1
        )
        basis = jnp.dot(windows, filters_ref[...], preferred_element_type=jnp.float32)
        basis_ref[d] = basis.astype(jnp.bfloat16)

    step = 256
    for j in range(0, templates, step):
        total = None
        for d in range(dets):
            for c in range(2):
                signal = jnp.dot(
                    basis_ref[d],
                    mixing_ref[c, :, j : j + step],
                    preferred_element_type=jnp.float32,
                )
                total = signal * signal if total is None else total + signal * signal
        score_ref[:, j : j + step] = 0.5 * total

    lanes = lax.broadcasted_iota(jnp.int32, (1, LANES), 1)
    for t in range(0, seg, LANES):
        tiles = [score_ref[t : t + LANES, j : j + LANES] for j in range(0, templates, LANES)]
        peak = functools.reduce(jnp.maximum, tiles)
        mass = functools.reduce(jnp.add, [jnp.exp(tile - peak) for tile in tiles])
        peak, mass = peak.T, mass.T
        top = jnp.max(peak, axis=0, keepdims=True)
        mass = jnp.sum(mass * jnp.exp(peak - top), axis=0, keepdims=True)
        line = top + jnp.log(mass)
        for bit in (1, 2, 4):
            line = jnp.where(
                (lanes & bit) == 0, pltpu.roll(line, LANES - bit, 1), pltpu.roll(line, bit, 1)
            )
        gather_ref[tmpl, :, t : t + LANES] = line

    sends = []
    for o in range(1, tmpl_count):
        send = pltpu.make_async_remote_copy(
            src_ref=gather_ref.at[tmpl],
            dst_ref=gather_ref.at[tmpl],
            send_sem=out_send.at[o],
            recv_sem=out_recv.at[o],
            device_id=(tm, lax.rem(tmpl + o, tmpl_count)),
            device_id_type=MESH,
        )
        send.start()
        sends.append(send)
    for send in sends:
        send.wait()
    parts = [gather_ref[i] for i in range(tmpl_count)]
    top = functools.reduce(jnp.maximum, parts)
    mass = functools.reduce(jnp.add, [jnp.exp(part - top) for part in parts])
    out_ref[...] = top + jnp.log(mass) - math.log(templates * tmpl_count)


def shards(tm_count, tmpl_count, strain, gate_lengths, filters, mixing):
    dets, seg = strain.shape
    _, taps, width = filters.shape
    templates = mixing.shape[2]
    hops = (taps + seg - 2) // seg
    out = pl.pallas_call(
        functools.partial(kernel, tm_count, tmpl_count),
        out_shape=jax.ShapeDtypeStruct((1, seg), jnp.float32),
        in_specs=[pl.BlockSpec(memory_space=pltpu.HBM)] * 4,
        out_specs=pl.BlockSpec(memory_space=pltpu.VMEM),
        scratch_shapes=[
            pltpu.VMEM((dets, seg), jnp.float32),
            pltpu.SMEM(gate_lengths.shape, jnp.int32),
            pltpu.VMEM((taps, width), jnp.bfloat16),
            pltpu.VMEM((width, 2, templates), jnp.bfloat16),
            pltpu.VMEM((2, width, templates), jnp.bfloat16),
            pltpu.VMEM((hops + 1, dets, seg), jnp.float32),
            pltpu.VMEM((dets, hops * seg + seg - LANES, LANES), jnp.bfloat16),
            pltpu.VMEM((dets, seg, width), jnp.bfloat16),
            pltpu.VMEM((seg, templates), jnp.float32),
            pltpu.VMEM((tmpl_count, 1, seg), jnp.float32),
            pltpu.SemaphoreType.DMA((3 + CHUNKS,)),
            pltpu.SemaphoreType.DMA((hops,)),
            pltpu.SemaphoreType.DMA((hops,)),
            pltpu.SemaphoreType.DMA((tmpl_count,)),
            pltpu.SemaphoreType.DMA((tmpl_count,)),
        ],
        compiler_params=pltpu.CompilerParams(
            collective_id=0, has_side_effects=True, vmem_limit_bytes=60 * 2**20
        ),
    )(strain, gate_lengths, filters, mixing)
    return out.reshape(seg)


def solution(mesh):
    body = functools.partial(shards, mesh.shape["tm"], mesh.shape["tmpl"])
    in_specs = (P(None, "tm"), P(), P("tmpl", None, None), P(None, None, "tmpl"))
    return jax.shard_map(body, mesh=mesh, in_specs=in_specs, out_specs=P("tm"), check_vma=False)
```

```python
import functools
import math

import jax
import jax.numpy as jnp
from jax import lax
from jax.experimental import pallas as pl
from jax.experimental.pallas import tpu as pltpu
from jax.sharding import PartitionSpec as P

MESH = pl.DeviceIdType.MESH
LANES = 128
ROWS = 8
CHUNKS = 4


def kernel(
    tm_count,
    tmpl_count,
    strain_hbm,
    gates_hbm,
    filters_hbm,
    mixing_hbm,
    out_ref,
    strain_ref,
    gates_ref,
    filters_ref,
    raw_ref,
    mixing_ref,
    ext_ref,
    hankel_ref,
    basis_ref,
    score_ref,
    gather_ref,
    load_sems,
    halo_send,
    halo_recv,
    out_send,
    out_recv,
    ready_sems,
):
    dets, seg = strain_ref.shape
    taps, width = filters_ref.shape
    templates = mixing_ref.shape[2]
    hops = (taps + seg - 2) // seg
    tm = lax.axis_index("tm")
    tmpl = lax.axis_index("tmpl")

    barrier = pltpu.get_barrier_semaphore()
    reach = sorted({o % tm_count for h in range(1, hops + 1) for o in (h, -h)} - {0})
    for o in reach:
        pl.semaphore_signal(
            barrier, inc=1, device_id=(lax.rem(tm + o, tm_count), tmpl), device_id_type=MESH
        )
    cores = 2
    chips = tmpl_count // cores
    chip, core = tmpl // cores, lax.rem(tmpl, cores)
    pl.semaphore_signal(barrier, inc=1, device_id=(tm, chip * cores + 1 - core), device_id_type=MESH)

    def tell(sem, distance):
        @pl.when(chip + distance < chips)
        def _():
            pl.semaphore_signal(
                sem, inc=1, device_id=(tm, tmpl + distance * cores), device_id_type=MESH
            )

        @pl.when(chip >= distance)
        def _():
            pl.semaphore_signal(
                sem, inc=1, device_id=(tm, tmpl - distance * cores), device_id_type=MESH
            )

    def told(distance):
        return (chip + distance < chips).astype(jnp.int32) + (chip >= distance).astype(jnp.int32)

    tell(barrier, 1)

    small = [
        pltpu.make_async_copy(strain_hbm, strain_ref, load_sems.at[0]),
        pltpu.make_async_copy(gates_hbm, gates_ref, load_sems.at[1]),
    ]
    chunk = width // CHUNKS
    mixing_loads = [
        pltpu.make_async_copy(
            mixing_hbm.at[pl.ds(i * chunk, chunk)],
            raw_ref.at[pl.ds(i * chunk, chunk)],
            load_sems.at[3 + i],
        )
        for i in range(CHUNKS)
    ]
    filters_load = pltpu.make_async_copy(filters_hbm.at[0], filters_ref, load_sems.at[2])
    for load in small + mixing_loads + [filters_load]:
        load.start()
    for load in small:
        load.wait()

    positions = tm * seg + lax.broadcasted_iota(jnp.int32, (1, seg), 1)
    passed = jnp.zeros((1, seg), jnp.int32)
    bound = jnp.int32(0)
    for g in range(gates_ref.shape[0]):
        bound = bound + gates_ref[g]
        passed = passed + (bound <= positions).astype(jnp.int32)
    keep = ((passed & 1) == 0).astype(jnp.float32)
    ext_ref[hops] = (strain_ref[...] * keep).astype(jnp.bfloat16).astype(jnp.float32)

    pl.semaphore_wait(barrier, len(reach) + 1 + told(1))
    halos = []
    for h in range(1, hops + 1):
        halo = pltpu.make_async_remote_copy(
            src_ref=ext_ref.at[hops],
            dst_ref=ext_ref.at[hops - h],
            send_sem=halo_send.at[h - 1],
            recv_sem=halo_recv.at[h - 1],
            device_id=(lax.rem(tm + h, tm_count), tmpl),
            device_id_type=MESH,
        )
        halo.start()
        halos.append(halo)
    tell(ready_sems.at[0], 1)

    per_piece = seg // LANES
    blocks = (hops + 1) * per_piece
    row = lax.broadcasted_iota(jnp.int32, (ROWS, LANES), 0)
    lane = lax.broadcasted_iota(jnp.int32, (ROWS, LANES), 1)
    inside = [lane - row + (r + ROWS) < LANES for r in range(0, LANES, ROWS)]

    def skewed(d, m):
        piece = m // per_piece
        at = (m % per_piece) * LANES
        line = ext_ref[piece, d : d + 1, at : at + LANES]
        if piece < hops:
            line = jnp.where(tm >= hops - piece, line, 0.0)
        wide = jnp.broadcast_to(line, (ROWS, LANES))
        return [
            pltpu.roll(wide, LANES - ROWS - r, 1, stride=1, stride_axis=0)
            for r in range(0, LANES, ROWS)
        ]

    def fill(d, first, last):
        now = skewed(d, first)
        for m in range(first, last):
            later = skewed(d, m + 1)
            tiles = [jnp.where(i, a, b) for i, a, b in zip(inside, now, later)]
            hankel_ref[d, m * LANES : (m + 1) * LANES, :] = jnp.concatenate(tiles, axis=0).astype(
                jnp.bfloat16
            )
            now = later

    own = hops * per_piece
    for d in range(dets):
        fill(d, own, blocks - 1)
    for i, load in enumerate(mixing_loads):
        load.wait()
        part = jnp.swapaxes(raw_ref[i * chunk : (i + 1) * chunk], 0, 1)
        for c in range(2):
            mixing_ref[c, i * chunk : (i + 1) * chunk, :] = part[c]
    filters_load.wait()
    for halo in halos:
        halo.wait()
    pl.semaphore_wait(ready_sems.at[0], told(1))
    distance = 2
    if distance < chips:
        tell(ready_sems.at[1], distance)
    for d in range(dets):
        fill(d, 0, own)
        windows = jnp.concatenate(
            [hankel_ref[d, k : k + seg, :] for k in range(0, taps, LANES)], axis=1
        )
        basis = jnp.dot(windows, filters_ref[...], preferred_element_type=jnp.float32)
        basis_ref[d] = basis.astype(jnp.bfloat16)

    step = 256
    for j in range(0, templates, step):
        total = None
        for d in range(dets):
            for c in range(2):
                signal = jnp.dot(
                    basis_ref[d],
                    mixing_ref[c, :, j : j + step],
                    preferred_element_type=jnp.float32,
                )
                total = signal * signal if total is None else total + signal * signal
        score_ref[:, j : j + step] = 0.5 * total

    lanes = lax.broadcasted_iota(jnp.int32, (1, LANES), 1)
    for t in range(0, seg, LANES):
        tiles = [score_ref[t : t + LANES, j : j + LANES] for j in range(0, templates, LANES)]
        peak = functools.reduce(jnp.maximum, tiles)
        mass = functools.reduce(jnp.add, [jnp.exp(tile - peak) for tile in tiles])
        peak, mass = peak.T, mass.T
        top = jnp.max(peak, axis=0, keepdims=True)
        mass = jnp.sum(mass * jnp.exp(peak - top), axis=0, keepdims=True)
        line = top + jnp.log(mass)
        for bit in (1, 2, 4):
            line = jnp.where(
                (lanes & bit) == 0, pltpu.roll(line, LANES - bit, 1), pltpu.roll(line, bit, 1)
            )
        gather_ref[tmpl, :, t : t + LANES] = line

    level = 1
    while distance < chips:
        pl.semaphore_wait(ready_sems.at[level], told(distance))
        distance, level = 2 * distance, level + 1
        if distance < chips:
            tell(ready_sems.at[level], distance)
    sends = []
    for o in range(1, tmpl_count):
        send = pltpu.make_async_remote_copy(
            src_ref=gather_ref.at[tmpl],
            dst_ref=gather_ref.at[tmpl],
            send_sem=out_send.at[o],
            recv_sem=out_recv.at[o],
            device_id=(tm, lax.rem(tmpl + o, tmpl_count)),
            device_id_type=MESH,
        )
        send.start()
        sends.append(send)
    for send in sends:
        send.wait()
    parts = [gather_ref[i] for i in range(tmpl_count)]
    top = functools.reduce(jnp.maximum, parts)
    mass = functools.reduce(jnp.add, [jnp.exp(part - top) for part in parts])
    out_ref[...] = top + jnp.log(mass)


def shards(tm_count, tmpl_count, strain, gate_lengths, filters, mixing):
    dets, seg = strain.shape
    _, taps, width = filters.shape
    templates = mixing.shape[2]
    hops = (taps + seg - 2) // seg
    out = pl.pallas_call(
        functools.partial(kernel, tm_count, tmpl_count),
        out_shape=jax.ShapeDtypeStruct((1, seg), jnp.float32),
        in_specs=[pl.BlockSpec(memory_space=pltpu.HBM)] * 4,
        out_specs=pl.BlockSpec(memory_space=pltpu.VMEM),
        scratch_shapes=[
            pltpu.VMEM((dets, seg), jnp.float32),
            pltpu.SMEM(gate_lengths.shape, jnp.int32),
            pltpu.VMEM((taps, width), jnp.bfloat16),
            pltpu.VMEM((width, 2, templates), jnp.bfloat16),
            pltpu.VMEM((2, width, templates), jnp.bfloat16),
            pltpu.VMEM((hops + 1, dets, seg), jnp.float32),
            pltpu.VMEM((dets, hops * seg + seg - LANES, LANES), jnp.bfloat16),
            pltpu.VMEM((dets, seg, width), jnp.bfloat16),
            pltpu.VMEM((seg, templates), jnp.float32),
            pltpu.VMEM((tmpl_count, 1, seg), jnp.float32),
            pltpu.SemaphoreType.DMA((3 + CHUNKS,)),
            pltpu.SemaphoreType.DMA((hops,)),
            pltpu.SemaphoreType.DMA((hops,)),
            pltpu.SemaphoreType.DMA((tmpl_count,)),
            pltpu.SemaphoreType.DMA((tmpl_count,)),
            pltpu.SemaphoreType.REGULAR((max(2, tmpl_count.bit_length()),)),
        ],
        compiler_params=pltpu.CompilerParams(
            collective_id=0, has_side_effects=True, vmem_limit_bytes=60 * 2**20
        ),
    )(strain, gate_lengths, filters, mixing)
    return out.reshape(seg) - math.log(templates * tmpl_count)


def solution(mesh):
    body = functools.partial(shards, mesh.shape["tm"], mesh.shape["tmpl"])
    in_specs = (P(None, "tm"), P(), P("tmpl", None, None), P(None, None, "tmpl"))
    return jax.shard_map(body, mesh=mesh, in_specs=in_specs, out_specs=P("tm"), check_vma=False)
```

```python
import functools
import math

import jax
import jax.numpy as jnp
from jax import lax
from jax.experimental import pallas as pl
from jax.experimental.pallas import tpu as pltpu
from jax.sharding import PartitionSpec as P

MESH = pl.DeviceIdType.MESH
LANES = 128
ROWS = 8
CHUNKS = 4


def kernel(
    tm_count,
    tmpl_count,
    strain_hbm,
    gates_hbm,
    filters_hbm,
    mixing_hbm,
    out_ref,
    strain_ref,
    gates_ref,
    filters_ref,
    raw_ref,
    mixing_ref,
    ext_ref,
    hankel_ref,
    basis_ref,
    score_ref,
    gather_ref,
    load_sems,
    halo_send,
    halo_recv,
    out_send,
    out_recv,
    ready_sems,
):
    dets, seg = strain_ref.shape
    taps, width = filters_ref.shape
    templates = mixing_ref.shape[2]
    hops = (taps + seg - 2) // seg
    tm = lax.axis_index("tm")
    tmpl = lax.axis_index("tmpl")

    barrier = pltpu.get_barrier_semaphore()
    for h in range(1, hops + 1):

        @pl.when(tm >= h)
        def _():
            pl.semaphore_signal(barrier, inc=1, device_id=(tm - h, tmpl), device_id_type=MESH)

    receivers = sum((tm + h < tm_count).astype(jnp.int32) for h in range(1, hops + 1))

    cores = 2
    chips = tmpl_count // cores
    chip, core = tmpl // cores, lax.rem(tmpl, cores)
    pl.semaphore_signal(barrier, inc=1, device_id=(tm, chip * cores + 1 - core), device_id_type=MESH)

    def tell(sem, distance):
        @pl.when(chip + distance < chips)
        def _():
            pl.semaphore_signal(
                sem, inc=1, device_id=(tm, tmpl + distance * cores), device_id_type=MESH
            )

        @pl.when(chip >= distance)
        def _():
            pl.semaphore_signal(
                sem, inc=1, device_id=(tm, tmpl - distance * cores), device_id_type=MESH
            )

    def told(distance):
        return (chip + distance < chips).astype(jnp.int32) + (chip >= distance).astype(jnp.int32)

    tell(barrier, 1)

    small = [
        pltpu.make_async_copy(strain_hbm, strain_ref, load_sems.at[0]),
        pltpu.make_async_copy(gates_hbm, gates_ref, load_sems.at[1]),
    ]
    chunk = width // CHUNKS
    mixing_loads = [
        pltpu.make_async_copy(
            mixing_hbm.at[pl.ds(i * chunk, chunk)],
            raw_ref.at[pl.ds(i * chunk, chunk)],
            load_sems.at[3 + i],
        )
        for i in range(CHUNKS)
    ]
    filters_load = pltpu.make_async_copy(filters_hbm.at[0], filters_ref, load_sems.at[2])
    for load in small + mixing_loads + [filters_load]:
        load.start()
    for load in small:
        load.wait()

    positions = tm * seg + lax.broadcasted_iota(jnp.int32, (1, seg), 1)
    passed = jnp.zeros((1, seg), jnp.int32)
    bound = jnp.int32(0)
    for g in range(gates_ref.shape[0]):
        bound = bound + gates_ref[g]
        passed = passed + (bound <= positions).astype(jnp.int32)
    keep = ((passed & 1) == 0).astype(jnp.float32)
    ext_ref[hops] = (strain_ref[...] * keep).astype(jnp.bfloat16).astype(jnp.float32)

    pl.semaphore_wait(barrier, receivers + 1 + told(1))
    halos = []
    for h in range(1, hops + 1):
        halo = pltpu.make_async_remote_copy(
            src_ref=ext_ref.at[hops],
            dst_ref=ext_ref.at[hops - h],
            send_sem=halo_send.at[h - 1],
            recv_sem=halo_recv.at[h - 1],
            device_id=(tm + h, tmpl),
            device_id_type=MESH,
        )
        pl.when(tm + h < tm_count)(halo.start)
        halos.append(halo)

        @pl.when(tm < h)
        def _():
            ext_ref[hops - h] = jnp.zeros((dets, seg), jnp.float32)

    tell(ready_sems.at[0], 1)

    per_piece = seg // LANES
    blocks = (hops + 1) * per_piece
    row = lax.broadcasted_iota(jnp.int32, (ROWS, LANES), 0)
    lane = lax.broadcasted_iota(jnp.int32, (ROWS, LANES), 1)
    inside = [lane - row + (r + ROWS) < LANES for r in range(0, LANES, ROWS)]

    def skewed(d, m):
        piece = m // per_piece
        at = (m % per_piece) * LANES
        line = ext_ref[piece, d : d + 1, at : at + LANES]
        wide = jnp.broadcast_to(line, (ROWS, LANES))
        return [
            pltpu.roll(wide, LANES - ROWS - r, 1, stride=1, stride_axis=0)
            for r in range(0, LANES, ROWS)
        ]

    def fill(d, first, last):
        now = skewed(d, first)
        for m in range(first, last):
            later = skewed(d, m + 1)
            tiles = [jnp.where(i, a, b) for i, a, b in zip(inside, now, later)]
            hankel_ref[d, m * LANES : (m + 1) * LANES, :] = jnp.concatenate(tiles, axis=0).astype(
                jnp.bfloat16
            )
            now = later

    own = hops * per_piece
    for d in range(dets):
        fill(d, own, blocks - 1)
    for i, load in enumerate(mixing_loads):
        load.wait()
        part = jnp.swapaxes(raw_ref[i * chunk : (i + 1) * chunk], 0, 1)
        for c in range(2):
            mixing_ref[c, i * chunk : (i + 1) * chunk, :] = part[c]
    filters_load.wait()
    for h, halo in enumerate(halos, 1):
        pl.when(tm + h < tm_count)(halo.wait_send)
        pl.when(tm >= h)(halo.wait_recv)
    pl.semaphore_wait(ready_sems.at[0], told(1))
    distance = 2
    if distance < chips:
        tell(ready_sems.at[1], distance)
    for d in range(dets):
        fill(d, 0, own)
        windows = jnp.concatenate(
            [hankel_ref[d, k : k + seg, :] for k in range(0, taps, LANES)], axis=1
        )
        basis = jnp.dot(windows, filters_ref[...], preferred_element_type=jnp.float32)
        basis_ref[d] = basis.astype(jnp.bfloat16)

    step = 256
    for j in range(0, templates, step):
        total = None
        for d in range(dets):
            for c in range(2):
                signal = jnp.dot(
                    basis_ref[d],
                    mixing_ref[c, :, j : j + step],
                    preferred_element_type=jnp.float32,
                )
                total = signal * signal if total is None else total + signal * signal
        score_ref[:, j : j + step] = 0.5 * total

    lanes = lax.broadcasted_iota(jnp.int32, (1, LANES), 1)
    for t in range(0, seg, LANES):
        tiles = [score_ref[t : t + LANES, j : j + LANES] for j in range(0, templates, LANES)]
        peak = functools.reduce(jnp.maximum, tiles)
        mass = functools.reduce(jnp.add, [jnp.exp(tile - peak) for tile in tiles])
        peak, mass = peak.T, mass.T
        top = jnp.max(peak, axis=0, keepdims=True)
        mass = jnp.sum(mass * jnp.exp(peak - top), axis=0, keepdims=True)
        line = top + jnp.log(mass)
        for bit in (1, 2, 4):
            line = jnp.where(
                (lanes & bit) == 0, pltpu.roll(line, LANES - bit, 1), pltpu.roll(line, bit, 1)
            )
        gather_ref[tmpl, :, t : t + LANES] = line

    level = 1
    while distance < chips:
        pl.semaphore_wait(ready_sems.at[level], told(distance))
        distance, level = 2 * distance, level + 1
        if distance < chips:
            tell(ready_sems.at[level], distance)
    sends = []
    for o in range(1, tmpl_count):
        send = pltpu.make_async_remote_copy(
            src_ref=gather_ref.at[tmpl],
            dst_ref=gather_ref.at[tmpl],
            send_sem=out_send.at[o],
            recv_sem=out_recv.at[o],
            device_id=(tm, lax.rem(tmpl + o, tmpl_count)),
            device_id_type=MESH,
        )
        send.start()
        sends.append(send)
    for send in sends:
        send.wait()
    parts = [gather_ref[i] for i in range(tmpl_count)]
    top = functools.reduce(jnp.maximum, parts)
    mass = functools.reduce(jnp.add, [jnp.exp(part - top) for part in parts])
    out_ref[...] = top + jnp.log(mass)


def shards(tm_count, tmpl_count, strain, gate_lengths, filters, mixing):
    dets, seg = strain.shape
    _, taps, width = filters.shape
    templates = mixing.shape[2]
    hops = (taps + seg - 2) // seg
    out = pl.pallas_call(
        functools.partial(kernel, tm_count, tmpl_count),
        out_shape=jax.ShapeDtypeStruct((1, seg), jnp.float32),
        in_specs=[pl.BlockSpec(memory_space=pltpu.HBM)] * 4,
        out_specs=pl.BlockSpec(memory_space=pltpu.VMEM),
        scratch_shapes=[
            pltpu.VMEM((dets, seg), jnp.float32),
            pltpu.SMEM(gate_lengths.shape, jnp.int32),
            pltpu.VMEM((taps, width), jnp.bfloat16),
            pltpu.VMEM((width, 2, templates), jnp.bfloat16),
            pltpu.VMEM((2, width, templates), jnp.bfloat16),
            pltpu.VMEM((hops + 1, dets, seg), jnp.float32),
            pltpu.VMEM((dets, hops * seg + seg - LANES, LANES), jnp.bfloat16),
            pltpu.VMEM((dets, seg, width), jnp.bfloat16),
            pltpu.VMEM((seg, templates), jnp.float32),
            pltpu.VMEM((tmpl_count, 1, seg), jnp.float32),
            pltpu.SemaphoreType.DMA((3 + CHUNKS,)),
            pltpu.SemaphoreType.DMA((hops,)),
            pltpu.SemaphoreType.DMA((hops,)),
            pltpu.SemaphoreType.DMA((tmpl_count,)),
            pltpu.SemaphoreType.DMA((tmpl_count,)),
            pltpu.SemaphoreType.REGULAR((max(2, tmpl_count.bit_length()),)),
        ],
        compiler_params=pltpu.CompilerParams(
            collective_id=0, has_side_effects=True, vmem_limit_bytes=60 * 2**20
        ),
    )(strain, gate_lengths, filters, mixing)
    return out.reshape(seg) - math.log(templates * tmpl_count)


def solution(mesh):
    body = functools.partial(shards, mesh.shape["tm"], mesh.shape["tmpl"])
    in_specs = (P(None, "tm"), P(), P("tmpl", None, None), P(None, None, "tmpl"))
    return jax.shard_map(body, mesh=mesh, in_specs=in_specs, out_specs=P("tm"), check_vma=False)
```
